512 devices in a mesh: row: 64 (over z, x_hi, core), rep: 8 (over y, x_lo).
Axes of the slice: x: 4 (x_hi: 2, x_lo: 2; x = x_hi * 2 + x_lo), y: 4, z: 16, core: 2. Of those that a mesh axis runs over, the one named last changes fastest.
Arguments:
- features: float32 [65536, 128], P(('row', 'rep')), may hold values from -6 to 6
- weight: float32 [128, 256], replicated, may hold values from -0.5 to 0.5
- bias: float32 [256], replicated, may hold values from -3 to 3
- adjacency: float32 [64, 8, 64, 128, 128], P('row', 'rep')
- tile_row: int32 [64, 8, 64], P('row', 'rep'), may hold values from 0 to 7
- tile_live: int32 [64, 8, 64], P('row', 'rep'), may hold values from 0 to 1
- node_live: int32 [65536], P(('row', 'rep')), may hold values 0 or 1
- cotangent: float32 [65536, 256], P(('row', 'rep'))
Outputs:
- activations: float32 [65536, 256], P(('row', 'rep'))
- weight_grad: float32 [128, 256], replicated
- bias_grad: float32 [256], replicated
The draws below stay inside these ranges and needn't reach their ends.
All inputs are finite; a program needn't handle non-finite values. No bound on the sum of `node_live` on one device may be relied on, other than what follows from the above.
Results may differ from the reference program's by a relative error of at most 0.0003.
Values sent between devices are 32-bit elements; how exact they have to be, the bound alone decides.
A program may use at most 64 MiB of HBM per device.

```python
import jax
import jax.numpy as jnp
from jax import lax

F_IN = 128
F_OUT = 256
TILE = 128
SECTIONS = 64
GROUPS = 8
NODES = 65536
FANIN = 8192


def draw_adjacency(key, part):
    first_key = jax.random.fold_in(key, 0)
    shape = (SECTIONS, GROUPS, SECTIONS, TILE, TILE)
    values = jax.random.uniform(first_key, shape, jnp.float32) * (4.0 / FANIN) ** 0.5
    return values


def draw_tile_live(key, part):
    shape = (SECTIONS, GROUPS, SECTIONS)
    scores = jax.random.randint(key, shape, 0, 1000)
    position = lax.broadcasted_iota(jnp.int32, shape, 0)
    limits = 300 + 650 * position // max(SECTIONS - 1, 1)
    return (scores < limits).astype(jnp.int32)


def draw_cotangent(key, part):
    first_key = jax.random.fold_in(key, 0)
    values = jax.random.normal(first_key, (NODES, F_OUT), jnp.float32)
    ramp = 1.0 + 2.0 * lax.broadcasted_iota(jnp.float32, (NODES, 1), 0) / (NODES - 1)
    return values * ramp / NODES ** 0.5


def touch_ends(result, stream_key, low, top_value):
    shape = result.shape
    index_at = [jax.random.randint(jax.random.fold_in(stream_key, axis), (), 0, shape[axis]) for axis in range(len(shape))]
    result = result.at[tuple(index_at)].set(low)
    longest = shape.index(max(shape))
    index_at[longest] = (index_at[longest] + 1) % shape[longest]
    return result.at[tuple(index_at)].set(top_value)


def steps_of(rng, dims, shards, smallest, top_value):
    def one(dim, blocks):
        draws = jax.random.uniform(jax.random.fold_in(jax.random.fold_in(rng, 6), dim), (blocks,), jnp.float32, smallest / len(shards), top_value / len(shards))
        return jnp.repeat(jnp.exp(draws), dims[dim] // blocks).reshape((-1,) + (1,) * (len(dims) - dim - 1))

    factor_of = one(*shards[0])
    for cut in shards[1:]:
        factor_of = factor_of * one(*cut)
    return factor_of


def normal_values(stream_key, shape, scale, limit, cuts=(), kind=jnp.bfloat16):
    gain = steps_of(stream_key, shape, cuts, -0.22, 0.18) if cuts else 1.0
    values = jax.random.normal(stream_key, shape, jnp.float32) * scale * gain
    return jnp.minimum(jnp.maximum(values, -limit), limit).astype(kind)


def setup_inputs(seed: int = 0) -> dict:
    arg_keys = jax.random.split(jax.random.key(seed), 9)
    return {
        "features": normal_values(arg_keys[0], (NODES, F_IN), 1.0, 6.0, ((0, 512),), jnp.float32),
        "weight": normal_values(arg_keys[1], (F_IN, F_OUT), F_IN ** -0.5, 0.5, (), jnp.float32),
        "bias": normal_values(arg_keys[2], (F_OUT,), 0.5, 3.0, (), jnp.float32),
        "adjacency": draw_adjacency(jax.random.fold_in(arg_keys[8], 71), 0),
        "tile_row": touch_ends(jax.random.randint(arg_keys[4], (SECTIONS, GROUPS, SECTIONS), 0, GROUPS), jax.random.fold_in(arg_keys[4], 1), 0, GROUPS - 1).astype(jnp.int32),
        "tile_live": draw_tile_live(jax.random.fold_in(arg_keys[8], 71), 0),
        "node_live": touch_ends((jax.random.randint(arg_keys[6], (NODES,), 0, 8) < 7).astype(jnp.int32), jax.random.fold_in(arg_keys[6], 1), 0, 1),
        "cotangent": draw_cotangent(jax.random.fold_in(arg_keys[8], 71), 0),
    }


def reference(features, weight, bias, adjacency, tile_row, tile_live, node_live, cotangent):
    blocks = features.reshape(SECTIONS, GROUPS, TILE, F_IN)
    group_ids = jnp.arange(GROUPS, dtype=jnp.int32)

    def partition_sum(inputs):
        part_tiles, part_rows, part_live = inputs
        products = jnp.einsum("csij,scjf->csif", part_tiles, blocks, precision=lax.Precision.HIGHEST)
        selector = part_live.astype(jnp.float32)[:, :, None] * (part_rows[:, :, None] == group_ids[None, None, :]).astype(jnp.float32)
        return jnp.einsum("csa,csif->aif", selector, products, precision=lax.Precision.HIGHEST)

    summed = lax.map(partition_sum, (adjacency, tile_row, tile_live))
    aggregated = summed.reshape(NODES, F_IN)
    preact = jnp.dot(aggregated, weight, precision=lax.Precision.HIGHEST) + bias
    node_mask = node_live.astype(jnp.float32)[:, None]
    sigmoid_value = jax.nn.sigmoid(preact)
    activations = preact * sigmoid_value * node_mask
    grad_preact = cotangent * node_mask * sigmoid_value * (1.0 + preact * (1.0 - sigmoid_value))
    weight_grad = jnp.dot(aggregated.T, grad_preact, precision=lax.Precision.HIGHEST)
    bias_grad = jnp.sum(grad_preact, axis=0)
    return activations, weight_grad, bias_grad
```

```python
import functools

import jax
import jax.numpy as jnp
from jax import lax
from jax.experimental import pallas as pl
from jax.experimental.pallas import tpu as pltpu
from jax.sharding import PartitionSpec as P

MESH = pl.DeviceIdType.MESH
F32 = jnp.float32
BF16 = jnp.bfloat16


def split(x):
    high = x.astype(BF16)
    return high, (x - high.astype(F32)).astype(BF16)


def arrived(ref, sem):
    pltpu.make_async_copy(ref, ref, sem).wait()


def kernel(
    feat,
    weight,
    bias,
    adj,
    trow,
    tlive,
    nlive,
    cot,
    act_out,
    wg_out,
    bg_out,
    gathered,
    tiles,
    wv,
    cv,
    acc,
    prods,
    incoming,
    av,
    part,
    plane_in,
    reduced,
    z_in,
    final,
    wsum,
    bpart,
    bplane,
    breduced,
    bz,
    bfinal,
    bsum,
    lsem,
    tsem,
    ssem,
    rsem,
    xs,
    xr,
    as_,
    ar,
    bs,
    br,
    osem,
):
    row = lax.axis_index("row")
    rep = lax.axis_index("rep")
    nz = lax.axis_size("row") // 4
    nrep = lax.axis_size("rep")
    nplane = 4 * nrep
    z, h, k = row // 4, (row // 2) % 2, row % 2
    d = 1 - 2 * k
    half = nz // 2

    def slab(t):
        return (z + t * d + nz) % nz

    def block(zz, hh, kk):
        return zz * 4 + hh * 2 + kk

    def at_device(r, p):
        return {"row": r, "rep": p}

    partner = at_device(block(z, h, 1 - k), rep)
    ahead = at_device(block(slab(1), h, k), rep)
    behind = at_device(block(slab(-1), h, k), rep)
    across = at_device(block(z, 1 - h, k), rep)

    barrier = pltpu.get_barrier_semaphore()

    def greet(dev):
        pl.semaphore_signal(barrier, inc=1, device_id=dev, device_id_type=MESH)

    greet(behind)
    greet(partner)
    greet(across)
    for j in range(1, nrep):
        greet(at_device(row, (rep + j) % nrep))

    tile_copy = pltpu.make_async_copy(adj, tiles, tsem)
    tile_copy.start()
    own_copy = pltpu.make_async_copy(feat, gathered.at[row], lsem.at[0])
    own_copy.start()
    w_copy = pltpu.make_async_copy(weight, wv, lsem.at[1])
    w_copy.start()
    c_copy = pltpu.make_async_copy(cot, cv, lsem.at[2])
    c_copy.start()
    pl.semaphore_wait(barrier, 3 + nrep - 1)

    def send(src, slot, dev):
        pltpu.make_async_remote_copy(
            src_ref=src,
            dst_ref=gathered.at[slot],
            send_sem=ssem,
            recv_sem=rsem.at[slot],
            device_id=dev,
            device_id_type=MESH,
        ).start()

    def take(slot):
        arrived(gathered.at[slot], rsem.at[slot])

    def group(zz):
        for j in range(4):
            s = zz * 4 + j
            fh, fl = split(gathered[s])
            right = jnp.concatenate([fh, fl], axis=1)
            right = jnp.concatenate([right, right], axis=0)
            ah, al = split(tiles[s])
            left = jnp.concatenate([ah, al], axis=1)
            both = jnp.dot(left, right, preferred_element_type=F32)
            prods[j] = both[:, :128] + both[:, 128:]
        picks = []
        for j in range(4):
            s = zz * 4 + j
            live = tlive[0, s].astype(F32)
            picks.append([jnp.where(trow[0, s] == a, live, 0.0) for a in range(8)])
        for a in range(8):
            total = acc[a]
            for j in range(4):
                total = total + prods[j] * picks[j][a]
            acc[a] = total

    send(feat, row, ahead)
    send(feat, row, partner)
    send(feat, row, across)
    acc[...] = jnp.zeros_like(acc)
    first = block(z, h, 1 - k)
    take(first)
    send(gathered.at[first], first, ahead)
    second = block(z, 1 - h, k)
    take(second)
    send(gathered.at[second], second, ahead)
    send(gathered.at[second], second, partner)
    third = block(z, 1 - h, 1 - k)
    take(third)
    send(gathered.at[third], third, ahead)

    def pass_on(t):
        zz = slab(-t)
        for at, (hh, kk) in enumerate(((h, k), (h, 1 - k), (1 - h, k), (1 - h, 1 - k))):
            slot = block(zz, hh, kk)
            take(slot)
            if at % 2 == 0:
                send(gathered.at[slot], slot, ahead)
            else:

                @pl.when(t < half - 1)
                def _():
                    send(gathered.at[slot], slot, ahead)

            send(gathered.at[slot], slot, partner)

    def take_slab(zz):
        for j in range(4):
            take(zz * 4 + j)

    pass_on(1)
    tile_copy.wait()
    own_copy.wait()
    group(z)

    def step(t, carry):
        pass_on(t)
        group(slab(1 - t))
        take_slab(slab(t - 1))
        group(slab(t - 1))
        return carry

    lax.fori_loop(2, half, step, 0)
    far = slab(half)
    for hh in (h, 1 - h):
        slot = block(far, hh, k)
        take(slot)
        send(gathered.at[slot], slot, partner)
    group(slab(1 - half))
    take_slab(slab(half - 1))
    group(slab(half - 1))
    for hh in (h, 1 - h):
        take(block(far, hh, 1 - k))
    group(far)

    for j in range(1, nrep):
        to = (rep + j) % nrep
        pltpu.make_async_remote_copy(
            src_ref=acc.at[to],
            dst_ref=incoming.at[j],
            send_sem=xs,
            recv_sem=xr,
            device_id=at_device(row, to),
            device_id_type=MESH,
        ).start()
    w_copy.wait()
    c_copy.wait()
    wh, wl = split(wv[...])
    live = jnp.transpose(jnp.broadcast_to(nlive[...].astype(F32), (128, 128)))
    mask = jnp.concatenate([live, live], axis=1)
    arrived(incoming.at[pl.ds(1, nrep - 1)], xr)
    agg = acc[rep]
    for j in range(1, nrep):
        agg = agg + incoming[j]
    ah, al = split(agg)
    pre = jnp.dot(
        jnp.concatenate([ah, al], axis=1),
        jnp.concatenate([wh, wh], axis=0),
        preferred_element_type=F32,
    )
    pre = pre + jnp.dot(ah, wl, preferred_element_type=F32) + bias[...]
    sig = jax.nn.sigmoid(pre)
    av[...] = pre * sig * mask
    act_copy = pltpu.make_async_copy(av, act_out, osem.at[0])
    act_copy.start()
    grad = cv[...] * mask * sig * (1.0 + pre * (1.0 - sig))
    gh, gl = split(grad)
    along = (((0,), (0,)), ((), ()))
    wpart = lax.dot_general(
        jnp.concatenate([ah, al], axis=0),
        jnp.concatenate([gh, gh], axis=0),
        along,
        preferred_element_type=F32,
    ) + lax.dot_general(ah, gl, along, preferred_element_type=F32)
    part[pl.ds(0, 16)] = wpart[:, :128].reshape(16, 8, 128)
    part[pl.ds(16, 16)] = wpart[:, 128:].reshape(16, 8, 128)
    bias_sum = jnp.sum(grad, axis=0, keepdims=True)
    bpart[...] = jnp.zeros_like(bpart)
    bpart[0:1] = bias_sum[:, :128]
    bpart[1:2] = bias_sum[:, 128:]

    me = (row % 4) * nrep + rep

    def plane_device(q):
        return at_device(z * 4 + q // nrep, q % nrep)

    def copy_to(src, dst, at, dev):
        pltpu.make_async_remote_copy(
            src_ref=src,
            dst_ref=dst,
            send_sem=as_.at[at],
            recv_sem=ar.at[at],
            device_id=dev,
            device_id_type=MESH,
        ).start()

    def bcopy(src, dst, at, dev):
        return pltpu.make_async_remote_copy(
            src_ref=src,
            dst_ref=dst,
            send_sem=bs.at[at],
            recv_sem=br.at[at],
            device_id=dev,
            device_id_type=MESH,
        )

    def scatter(j, carry):
        q = (me + j) % nplane
        copy_to(part.at[q], plane_in.at[j], 0, plane_device(q))
        return carry

    lax.fori_loop(1, nplane, scatter, 0)

    @pl.when(me != 0)
    def _():
        bcopy(bpart, bplane.at[me], 0, plane_device(0)).start()

    arrived(plane_in.at[pl.ds(1, nplane - 1)], ar.at[0])
    total = part[me]
    for j in range(1, nplane):
        total = total + plane_in[j]
    reduced[...] = total
    z_in[z] = total

    def along_z(j, carry):
        zz = (z + j) % nz
        copy_to(reduced, z_in.at[z], 1, at_device(zz * 4 + row % 4, rep))
        return carry

    lax.fori_loop(1, nz, along_z, 0)

    @pl.when(me == 0)
    def _():
        arrived(bplane.at[pl.ds(1, nplane - 1)], br.at[0])
        btotal = bpart[...]
        for j in range(1, nplane):
            btotal = btotal + bplane[j]
        breduced[...] = btotal
        bz[z] = btotal

        def balong(j, carry):
            zz = (z + j) % nz
            bcopy(breduced, bz.at[z], 1, at_device(zz * 4 + row % 4, rep)).start()
            return carry

        lax.fori_loop(1, nz, balong, 0)

    arrived(z_in.at[pl.ds(1, nz - 1)], ar.at[1])
    total = z_in[0]
    for j in range(1, nz):
        total = total + z_in[j]
    final[...] = total
    wsum[me] = total

    def gather(j, carry):
        q = (me + j) % nplane
        copy_to(final, wsum.at[me], 2, plane_device(q))
        return carry

    lax.fori_loop(1, nplane, gather, 0)

    @pl.when(me == 0)
    def _():
        arrived(bz.at[pl.ds(1, nz - 1)], br.at[1])
        btotal = bz[0]
        for j in range(1, nz):
            btotal = btotal + bz[j]
        bfinal[...] = btotal
        bsum[...] = btotal

        def bgather(j, carry):
            bcopy(bfinal, bsum, 2, plane_device(j)).start()
            return carry

        lax.fori_loop(1, nplane, bgather, 0)

    arrived(wsum.at[pl.ds(1, nplane - 1)], ar.at[2])
    wg_out[:, :128] = wsum[pl.ds(0, 16)].reshape(128, 128)
    wg_out[:, 128:] = wsum[pl.ds(16, 16)].reshape(128, 128)

    @pl.when(me != 0)
    def _():
        arrived(bsum, br.at[2])
        arrived(bpart, bs.at[0])

    bg_out[:, :128] = bsum[0:1]
    bg_out[:, 128:] = bsum[1:2]

    @pl.when(me == 0)
    def _():
        arrived(bz.at[pl.ds(1, nz - 1)], bs.at[1])
        arrived(bplane.at[pl.ds(1, nplane - 1)], bs.at[2])

    sent = nz * 4 - 1
    arrived(gathered.at[pl.ds(0, sent)], ssem)
    arrived(incoming.at[pl.ds(1, nrep - 1)], xs)
    arrived(plane_in.at[pl.ds(1, nplane - 1)], as_.at[0])
    arrived(z_in.at[pl.ds(1, nz - 1)], as_.at[1])
    arrived(plane_in.at[pl.ds(1, nplane - 1)], as_.at[2])
    act_copy.wait()


def local(features, weight, bias, adjacency, tile_row, tile_live, node_live, cotangent):
    count = adjacency.shape[2]
    nrep = lax.axis_size("rep")
    nplane = 4 * nrep
    nz = lax.axis_size("row") // 4
    hbm = pl.BlockSpec(memory_space=pltpu.HBM)
    vmem = pl.BlockSpec(memory_space=pltpu.VMEM)
    smem = pl.BlockSpec(memory_space=pltpu.SMEM)
    dma = pltpu.SemaphoreType.DMA
    act, wg, bg = pl.pallas_call(
        kernel,
        out_shape=(
            jax.ShapeDtypeStruct((128, 256), F32),
            jax.ShapeDtypeStruct((128, 256), F32),
            jax.ShapeDtypeStruct((1, 256), F32),
        ),
        in_specs=[hbm, hbm, vmem, hbm, smem, smem, vmem, hbm],
        out_specs=(hbm, vmem, vmem),
        scratch_shapes=[
            pltpu.VMEM((count, 128, 128), F32),
            pltpu.VMEM((count, 128, 128), F32),
            pltpu.VMEM((128, 256), F32),
            pltpu.VMEM((128, 256), F32),
            pltpu.VMEM((nrep, 128, 128), F32),
            pltpu.VMEM((4, 128, 128), F32),
            pltpu.VMEM((nrep, 128, 128), F32),
            pltpu.VMEM((128, 256), F32),
            pltpu.VMEM((nplane, 8, 128), F32),
            pltpu.VMEM((nplane, 8, 128), F32),
            pltpu.VMEM((8, 128), F32),
            pltpu.VMEM((nz, 8, 128), F32),
            pltpu.VMEM((8, 128), F32),
            pltpu.VMEM((nplane, 8, 128), F32),
            pltpu.VMEM((8, 128), F32),
            pltpu.VMEM((nplane, 8, 128), F32),
            pltpu.VMEM((8, 128), F32),
            pltpu.VMEM((nz, 8, 128), F32),
            pltpu.VMEM((8, 128), F32),
            pltpu.VMEM((8, 128), F32),
            dma((3,)),
            dma,
            dma,
            dma((count,)),
            dma,
            dma,
            dma((3,)),
            dma((3,)),
            dma((3,)),
            dma((3,)),
            dma((1,)),
        ],
        compiler_params=pltpu.CompilerParams(
            collective_id=0, has_side_effects=True, vmem_limit_bytes=48 * 1024 * 1024
        ),
    )(
        features,
        weight,
        bias.reshape(1, 256),
        adjacency.reshape(count, 128, 128),
        tile_row.reshape(1, count),
        tile_live.reshape(1, count),
        node_live.reshape(1, 128),
        cotangent,
    )
    return act, wg, bg.reshape(256)


def solution(mesh):
    placed = (
        P(("row", "rep"), None),
        P(),
        P(),
        P("row", "rep", None, None, None),
        P("row", "rep", None),
        P("row", "rep", None),
        P(("row", "rep")),
        P(("row", "rep"), None),
    )
    return jax.shard_map(
        local,
        mesh=mesh,
        in_specs=placed,
        out_specs=(P(("row", "rep"), None), P(), P()),
        check_vma=False,
    )
```

```python
import functools

import jax
import jax.numpy as jnp
from jax import lax
from jax.experimental import pallas as pl
from jax.experimental.pallas import tpu as pltpu
from jax.sharding import PartitionSpec as P

MESH = pl.DeviceIdType.MESH
F32 = jnp.float32
CHUNKS = 1
PLANE = sorted(
    ((dx, dy, dk) for dx in range(4) for dy in range(4) for dk in range(2)),
    key=lambda d: -(min(d[0], 4 - d[0]) + min(d[1], 4 - d[1])) * 2 - d[2],
)[:-1]
BF16 = jnp.bfloat16


def split(x):
    high = x.astype(BF16)
    return high, (x - high.astype(F32)).astype(BF16)


def arrived(ref, sem):
    pltpu.make_async_copy(ref, ref, sem).wait()


def kernel(
    feat,
    weight,
    bias,
    adj,
    trow,
    tlive,
    nlive,
    cot,
    act_out,
    wg_out,
    bg_out,
    gathered,
    tiles,
    wv,
    cv,
    acc,
    prods,
    incoming,
    av,
    part,
    plane_in,
    reduced,
    z_in,
    final,
    wsum,
    bpart,
    bplane,
    breduced,
    bz,
    bfinal,
    bsum,
    row_s,
    live_s,
    bias_v,
    node_v,
    ready,
    lsem,
    tsem,
    ssem,
    rsem,
    xs,
    xr,
    as_,
    ar,
    bs,
    br,
    osem,
):
    row = lax.axis_index("row")
    rep = lax.axis_index("rep")
    nz = lax.axis_size("row") // 4
    nrep = lax.axis_size("rep")
    nplane = 4 * nrep
    rows = 128 // CHUNKS
    z, h, k = row // 4, (row // 2) % 2, row % 2
    d = 1 - 2 * k

    def slab(t):
        return (z + t * d + nz) % nz

    def block(zz, hh, kk):
        return zz * 4 + hh * 2 + kk

    def at_device(r, p):
        return {"row": r, "rep": p}

    partner = at_device(block(z, h, 1 - k), rep)
    ahead = {t: at_device(block(slab(t), h, k), rep) for t in (1, 2)}
    across = at_device(block(z, 1 - h, k), rep)

    barrier = pltpu.get_barrier_semaphore()

    def greet(dev):
        pl.semaphore_signal(barrier, inc=1, device_id=dev, device_id_type=MESH)

    for t in (1, 2):
        greet(at_device(block(slab(-t), h, k), rep))
    greet(partner)
    greet(across)
    y, side_x = rep // 2, rep % 2
    ny = nrep // 2
    beside = [at_device(row, ((y + dy) % ny) * 2 + side_x) for dy in (1, 3)]
    for dev in beside:
        greet(dev)
    greet(at_device(row, y * 2 + 1 - side_x))

    own_copy = pltpu.make_async_copy(feat, gathered.at[row], lsem.at[0])
    own_copy.start()
    row_copy = pltpu.make_async_copy(trow, row_s, lsem.at[3])
    row_copy.start()
    live_copy = pltpu.make_async_copy(tlive, live_s, lsem.at[4])
    live_copy.start()
    tile_copy = pltpu.make_async_copy(adj, tiles, tsem)
    tile_copy.start()
    w_copy = pltpu.make_async_copy(weight, wv, lsem.at[1])
    w_copy.start()
    c_copy = pltpu.make_async_copy(cot, cv, lsem.at[2])
    c_copy.start()
    bias_copy = pltpu.make_async_copy(bias, bias_v, lsem.at[5])
    bias_copy.start()
    node_copy = pltpu.make_async_copy(nlive, node_v, lsem.at[6])
    node_copy.start()
    pl.semaphore_wait(barrier, 7)

    def tell(at):
        for dev in beside:
            pl.semaphore_signal(ready.at[at], inc=1, device_id=dev, device_id_type=MESH)

    own_copy.wait()

    def piece(slot, c):
        return gathered.at[slot, pl.ds(c * rows, rows)]

    def push(src, slot, c, dev):
        pltpu.make_async_remote_copy(
            src_ref=src,
            dst_ref=piece(slot, c),
            send_sem=ssem,
            recv_sem=rsem.at[slot, c],
            device_id=dev,
            device_id_type=MESH,
        ).start()

    def first(c, dev):
        push(piece(row, c), row, c, dev)

    def send(slot, c, dev):
        push(piece(slot, c), slot, c, dev)

    def take(slot, c):
        arrived(piece(slot, c), rsem.at[slot, c])

    def take_all(slot):
        for c in range(CHUNKS):
            take(slot, c)

    def pair(zz, hh):
        base = zz * 4 + hh * 2
        for j in range(2):
            fh, fl = split(gathered[base + j])
            right = jnp.concatenate([fh, fl], axis=1)
            right = jnp.concatenate([right, right], axis=0)
            ah, al = split(tiles[base + j])
            left = jnp.concatenate([ah, al], axis=1)
            both = jnp.dot(left, right, preferred_element_type=F32)
            prods[j] = both[:, :128] + both[:, 128:]
        picks = []
        for j in range(2):
            live = live_s[0, base + j].astype(F32)
            target = row_s[0, base + j]
            picks.append([jnp.where(target == a, live, 0.0) for a in range(8)])
        for a in range(8):
            acc[a] = acc[a] + (prods[0] * picks[0][a] + prods[1] * picks[1][a])

    def duo(t, hh):
        for kk in range(2):
            take_all(block(slab(t), hh, kk))

        def side(i, carry):
            pair(slab(t * (2 * i - 1)), hh)
            return carry

        lax.fori_loop(0, 2, side, 0)

    other = 1 - k

    def ring(t):
        for c in range(CHUNKS):
            for kk, end in ((k, 8), (other, 7)):
                if t > end:
                    continue
                slot = block(slab(-t), h, kk)
                take(slot, c)
                if t % 2 == 0:
                    for hop in (2, 1):
                        if t + hop <= end:
                            send(slot, c, ahead[hop])
                send(slot, c, across)
                send(slot, c, partner)

    def crossed(t):
        for c in range(CHUNKS):
            for kk, end in ((k, 8), (other, 7)):
                if t > end or (t == 0 and kk is other):
                    continue
                slot = block(slab(-t), 1 - h, kk)
                take(slot, c)
                send(slot, c, partner)

    for c in range(CHUNKS):
        first(c, partner)
        for hop in (2, 1):
            first(c, ahead[hop])
        first(c, across)
    tell(0)
    acc[...] = jnp.zeros_like(acc)
    mine = block(z, h, other)
    for c in range(CHUNKS):
        take(mine, c)
        for hop in (2, 1):
            send(mine, c, ahead[hop])
    tile_copy.wait()
    row_copy.wait()
    live_copy.wait()
    ring(2)
    pl.semaphore_wait(ready.at[0], 2)
    tell(1)
    pair(z, h)
    ring(1)
    duo(2, h)
    for t in (4, 6):
        ring(t)
        duo(t - 3, h)
        ring(t - 1)
        duo(t, h)
    ring(8)
    ring(7)
    for t in (0, 2, 1, 4, 3):
        crossed(t)
    duo(5, h)
    take_all(block(z, 1 - h, other))
    pair(z, 1 - h)
    duo(2, 1 - h)
    duo(1, 1 - h)
    for t in (6, 5):
        crossed(t)
    duo(7, h)
    take_all(block(slab(8), h, other))
    pair(slab(8), h)
    duo(4, 1 - h)
    crossed(8)
    crossed(7)
    for t in (3, 6, 5, 7):
        duo(t, 1 - h)
    take_all(block(slab(8), 1 - h, other))
    pair(slab(8), 1 - h)

    pl.semaphore_wait(ready.at[1], 2)
    for dy, dx in ((2, 1), (1, 1), (3, 1), (0, 1), (2, 0), (1, 0), (3, 0)):
        to = ((y + dy) % ny) * 2 + (side_x + dx) % 2
        pltpu.make_async_remote_copy(
            src_ref=acc.at[to],
            dst_ref=incoming.at[dy * 2 + dx],
            send_sem=xs,
            recv_sem=xr,
            device_id=at_device(row, to),
            device_id_type=MESH,
        ).start()
    w_copy.wait()
    c_copy.wait()
    bias_copy.wait()
    node_copy.wait()
    wh, wl = split(wv[...])
    live = jnp.transpose(jnp.broadcast_to(node_v[...].astype(F32), (128, 128)))
    mask = jnp.concatenate([live, live], axis=1)
    arrived(incoming.at[pl.ds(1, nrep - 1)], xr)
    agg = acc[rep]
    for j in range(1, nrep):
        agg = agg + incoming[j]
    ah, al = split(agg)
    pre = jnp.dot(
        jnp.concatenate([ah, al], axis=1),
        jnp.concatenate([wh, wh], axis=0),
        preferred_element_type=F32,
    )
    pre = pre + jnp.dot(ah, wl, preferred_element_type=F32) + bias_v[...]
    sig = jax.nn.sigmoid(pre)
    av[...] = pre * sig * mask
    act_copy = pltpu.make_async_copy(av, act_out, osem.at[0])
    act_copy.start()
    grad = cv[...] * mask * sig * (1.0 + pre * (1.0 - sig))
    gh, gl = split(grad)
    along = (((0,), (0,)), ((), ()))
    wpart = lax.dot_general(
        jnp.concatenate([ah, al], axis=0),
        jnp.concatenate([gh, gh], axis=0),
        along,
        preferred_element_type=F32,
    ) + lax.dot_general(ah, gl, along, preferred_element_type=F32)
    part[pl.ds(0, 16)] = wpart[:, :128].reshape(16, 8, 128)
    part[pl.ds(16, 16)] = wpart[:, 128:].reshape(16, 8, 128)
    bias_sum = jnp.sum(grad, axis=0, keepdims=True)
    bpart[...] = jnp.zeros_like(bpart)
    bpart[0:1] = bias_sum[:, :128]
    bpart[1:2] = bias_sum[:, 128:]

    me = (row % 4) * nrep + rep

    x = h * 2 + side_x
    xs_at = [(x + dx) % 4 for dx in range(4)]
    row_at = [[z * 4 + xx // 2 * 2 + (k + dk) % 2 for dk in range(2)] for xx in xs_at]
    rep_at = [[(y + dy) % ny * 2 + xx % 2 for dy in range(4)] for xx in xs_at]

    def plane_peers():
        for j, (dx, dy, dk) in enumerate(PLANE):
            r, p = row_at[dx][dk], rep_at[dx][dy]
            yield j + 1, (r - z * 4) * nrep + p, at_device(r, p)

    z_far = sorted(range(1, nz), key=lambda j: -min(j, nz - j))

    def z_peers():
        for j in z_far:
            yield at_device((z + j) % nz * 4 + row % 4, rep)

    def copy_to(src, dst, at, dev):
        pltpu.make_async_remote_copy(
            src_ref=src,
            dst_ref=dst,
            send_sem=as_.at[at],
            recv_sem=ar.at[at],
            device_id=dev,
            device_id_type=MESH,
        ).start()

    def bcopy(src, dst, at, dev):
        return pltpu.make_async_remote_copy(
            src_ref=src,
            dst_ref=dst,
            send_sem=bs.at[at],
            recv_sem=br.at[at],
            device_id=dev,
            device_id_type=MESH,
        )

    for j, q, dev in plane_peers():
        copy_to(part.at[q], plane_in.at[j], 0, dev)

    @pl.when(me != 0)
    def _():
        bcopy(bpart, bplane.at[me], 0, at_device(z * 4, 0)).start()

    arrived(plane_in.at[pl.ds(1, nplane - 1)], ar.at[0])
    total = part[me]
    for j in range(1, nplane):
        total = total + plane_in[j]
    reduced[...] = total
    z_in[z] = total

    for dev in z_peers():
        copy_to(reduced, z_in.at[z], 1, dev)

    @pl.when(me == 0)
    def _():
        arrived(bplane.at[pl.ds(1, nplane - 1)], br.at[0])
        btotal = bpart[...]
        for j in range(1, nplane):
            btotal = btotal + bplane[j]
        breduced[...] = btotal
        bz[z] = btotal

        def balong(j, carry):
            zz = (z + j) % nz
            bcopy(breduced, bz.at[z], 1, at_device(zz * 4 + row % 4, rep)).start()
            return carry

        lax.fori_loop(1, nz, balong, 0)

    arrived(z_in.at[pl.ds(1, nz - 1)], ar.at[1])
    total = z_in[0]
    for j in range(1, nz):
        total = total + z_in[j]
    final[...] = total
    wsum[me] = total

    for j, q, dev in plane_peers():
        copy_to(final, wsum.at[me], 2, dev)

    @pl.when(me == 0)
    def _():
        arrived(bz.at[pl.ds(1, nz - 1)], br.at[1])
        btotal = bz[0]
        for j in range(1, nz):
            btotal = btotal + bz[j]
        bfinal[...] = btotal
        bsum[...] = btotal

        def bgather(j, carry):
            bcopy(bfinal, bsum, 2, at_device(z * 4 + j // nrep, j % nrep)).start()
            return carry

        lax.fori_loop(1, nplane, bgather, 0)

    arrived(wsum.at[pl.ds(1, nplane - 1)], ar.at[2])
    wg_out[:, :128] = wsum[pl.ds(0, 16)].reshape(128, 128)
    wg_out[:, 128:] = wsum[pl.ds(16, 16)].reshape(128, 128)

    @pl.when(me != 0)
    def _():
        arrived(bsum, br.at[2])
        arrived(bpart, bs.at[0])

    bg_out[:, :128] = bsum[0:1]
    bg_out[:, 128:] = bsum[1:2]

    @pl.when(me == 0)
    def _():
        arrived(bz.at[pl.ds(1, nz - 1)], bs.at[1])
        arrived(bplane.at[pl.ds(1, nplane - 1)], bs.at[2])

    sent = nz * 4 - 1
    arrived(gathered.at[pl.ds(0, sent)], ssem)
    arrived(incoming.at[pl.ds(1, nrep - 1)], xs)
    arrived(plane_in.at[pl.ds(1, nplane - 1)], as_.at[0])
    arrived(z_in.at[pl.ds(1, nz - 1)], as_.at[1])
    arrived(plane_in.at[pl.ds(1, nplane - 1)], as_.at[2])
    act_copy.wait()


def writer(act, wg, bg, act_out, wg_out, bg_out, sems):
    copies = [
        pltpu.make_async_copy(src, dst, sems.at[i])
        for i, (src, dst) in enumerate(((act, act_out), (wg, wg_out), (bg, bg_out)))
    ]
    for copy in copies:
        copy.start()
    for copy in copies:
        copy.wait()


def write_out(act, wg, bg):
    vmem = pl.BlockSpec(memory_space=pltpu.VMEM)
    hbm = pl.BlockSpec(memory_space=pltpu.HBM)
    act, wg, bg = pl.pallas_call(
        writer,
        out_shape=tuple(jax.ShapeDtypeStruct(x.shape, F32) for x in (act, wg, bg)),
        in_specs=[vmem] * 3,
        out_specs=(hbm,) * 3,
        scratch_shapes=[pltpu.SemaphoreType.DMA((3,))],
        compiler_params=pltpu.CompilerParams(vmem_limit_bytes=4 * 1024 * 1024),
    )(act, wg, bg)
    return act, wg, bg.reshape(256)


def local(features, weight, bias, adjacency, tile_row, tile_live, node_live, cotangent):
    count = adjacency.shape[2]
    nrep = lax.axis_size("rep")
    nplane = 4 * nrep
    nz = lax.axis_size("row") // 4
    hbm = pl.BlockSpec(memory_space=pltpu.HBM)
    vmem = pl.BlockSpec(memory_space=pltpu.VMEM)
    dma = pltpu.SemaphoreType.DMA
    act, wg, bg = pl.pallas_call(
        kernel,
        out_shape=(
            jax.ShapeDtypeStruct((128, 256), F32),
            jax.ShapeDtypeStruct((128, 256), F32),
            jax.ShapeDtypeStruct((1, 256), F32),
        ),
        in_specs=[hbm] * 8,
        out_specs=(hbm, vmem, vmem),
        scratch_shapes=[
            pltpu.VMEM((count, 128, 128), F32),
            pltpu.VMEM((count, 128, 128), F32),
            pltpu.VMEM((128, 256), F32),
            pltpu.VMEM((128, 256), F32),
            pltpu.VMEM((nrep, 128, 128), F32),
            pltpu.VMEM((2, 128, 128), F32),
            pltpu.VMEM((nrep, 128, 128), F32),
            pltpu.VMEM((128, 256), F32),
            pltpu.VMEM((nplane, 8, 128), F32),
            pltpu.VMEM((nplane, 8, 128), F32),
            pltpu.VMEM((8, 128), F32),
            pltpu.VMEM((nz, 8, 128), F32),
            pltpu.VMEM((8, 128), F32),
            pltpu.VMEM((nplane, 8, 128), F32),
            pltpu.VMEM((8, 128), F32),
            pltpu.VMEM((nplane, 8, 128), F32),
            pltpu.VMEM((8, 128), F32),
            pltpu.VMEM((nz, 8, 128), F32),
            pltpu.VMEM((8, 128), F32),
            pltpu.VMEM((8, 128), F32),
            pltpu.SMEM((1, count), jnp.int32),
            pltpu.SMEM((1, count), jnp.int32),
            pltpu.VMEM((1, 256), F32),
            pltpu.VMEM((1, 128), jnp.int32),
            pltpu.SemaphoreType.REGULAR((2,)),
            dma((7,)),
            dma,
            dma,
            dma((count, CHUNKS)),
            dma,
            dma,
            dma((3,)),
            dma((3,)),
            dma((3,)),
            dma((3,)),
            dma((1,)),
        ],
        compiler_params=pltpu.CompilerParams(
            collective_id=0, has_side_effects=True, vmem_limit_bytes=24 * 1024 * 1024
        ),
    )(
        *(
            pltpu.with_memory_space_constraint(x, pltpu.HBM)
            for x in (
                features,
                weight,
                bias.reshape(1, 256),
                adjacency.reshape(count, 128, 128),
                tile_row.reshape(1, count),
                tile_live.reshape(1, count),
                node_live.reshape(1, 128),
                cotangent,
            )
        )
    )
    return write_out(act, wg, bg)


def solution(mesh):
    placed = (
        P(("row", "rep"), None),
        P(),
        P(),
        P("row", "rep", None, None, None),
        P("row", "rep", None),
        P("row", "rep", None),
        P(("row", "rep")),
        P(("row", "rep"), None),
    )
    return jax.shard_map(
        local,
        mesh=mesh,
        in_specs=placed,
        out_specs=(P(("row", "rep"), None), P(), P()),
        check_vma=False,
    )
```

```python
import functools

import jax
import jax.numpy as jnp
from jax import lax
from jax.experimental import pallas as pl
from jax.experimental.pallas import tpu as pltpu
from jax.sharding import PartitionSpec as P

MESH = pl.DeviceIdType.MESH
F32 = jnp.float32
CHUNKS = 1
PLANE = sorted(
    ((dx, dy, dk) for dx in range(4) for dy in range(4) for dk in range(2)),
    key=lambda d: -(min(d[0], 4 - d[0]) + min(d[1], 4 - d[1])) * 2 - d[2],
)[:-1]
BF16 = jnp.bfloat16


def split(x):
    high = x.astype(BF16)
    return high, (x - high.astype(F32)).astype(BF16)


def arrived(ref, sem):
    pltpu.make_async_copy(ref, ref, sem).wait()


def kernel(
    feat,
    weight,
    bias,
    adj,
    trow,
    tlive,
    nlive,
    cot,
    act_out,
    wg_out,
    bg_out,
    gathered,
    tiles,
    wv,
    cv,
    acc,
    prods,
    incoming,
    av,
    part,
    plane_in,
    reduced,
    z_in,
    final,
    wsum,
    bpart,
    bplane,
    breduced,
    bz,
    bfinal,
    bsum,
    row_s,
    live_s,
    bias_v,
    node_v,
    ready,
    lsem,
    tsem,
    ssem,
    rsem,
    xs,
    xr,
    as_,
    ar,
    bs,
    br,
    osem,
):
    row = lax.axis_index("row")
    rep = lax.axis_index("rep")
    nz = lax.axis_size("row") // 4
    nrep = lax.axis_size("rep")
    nplane = 4 * nrep
    rows = 128 // CHUNKS
    z, h, k = row // 4, (row // 2) % 2, row % 2
    d = 1 - 2 * k

    def slab(t):
        return (z + t * d + nz) % nz

    def block(zz, hh, kk):
        return zz * 4 + hh * 2 + kk

    def at_device(r, p):
        return {"row": r, "rep": p}

    partner = at_device(block(z, h, 1 - k), rep)
    ahead = {t: at_device(block(slab(t), h, k), rep) for t in (1, 2)}
    across = at_device(block(z, 1 - h, k), rep)

    barrier = pltpu.get_barrier_semaphore()

    def greet(dev):
        pl.semaphore_signal(barrier, inc=1, device_id=dev, device_id_type=MESH)

    for t in (1, 2):
        greet(at_device(block(slab(-t), h, k), rep))
    greet(partner)
    greet(across)
    y, side_x = rep // 2, rep % 2
    ny = nrep // 2
    beside = [at_device(row, ((y + dy) % ny) * 2 + side_x) for dy in (1, 3)]
    for dev in beside:
        greet(dev)
    greet(at_device(row, y * 2 + 1 - side_x))

    own_copy = pltpu.make_async_copy(feat, gathered.at[row], lsem.at[0])
    own_copy.start()
    row_copy = pltpu.make_async_copy(trow, row_s, lsem.at[3])
    row_copy.start()
    live_copy = pltpu.make_async_copy(tlive, live_s, lsem.at[4])
    live_copy.start()
    tile_copy = pltpu.make_async_copy(adj, tiles, tsem)
    tile_copy.start()
    w_copy = pltpu.make_async_copy(weight, wv, lsem.at[1])
    w_copy.start()
    c_copy = pltpu.make_async_copy(cot, cv, lsem.at[2])
    c_copy.start()
    bias_copy = pltpu.make_async_copy(bias, bias_v, lsem.at[5])
    bias_copy.start()
    node_copy = pltpu.make_async_copy(nlive, node_v, lsem.at[6])
    node_copy.start()
    pl.semaphore_wait(barrier, 7)

    def tell(at):
        for dev in beside:
            pl.semaphore_signal(ready.at[at], inc=1, device_id=dev, device_id_type=MESH)

    own_copy.wait()

    def piece(slot, c):
        return gathered.at[slot, pl.ds(c * rows, rows)]

    def push(src, slot, c, dev):
        pltpu.make_async_remote_copy(
            src_ref=src,
            dst_ref=piece(slot, c),
            send_sem=ssem,
            recv_sem=rsem.at[slot, c],
            device_id=dev,
            device_id_type=MESH,
        ).start()

    def first(c, dev):
        push(piece(row, c), row, c, dev)

    def send(slot, c, dev):
        push(piece(slot, c), slot, c, dev)

    def take(slot, c):
        arrived(piece(slot, c), rsem.at[slot, c])

    def take_all(slot):
        for c in range(CHUNKS):
            take(slot, c)

    def pair(zz, hh):
        base = zz * 4 + hh * 2
        for j in range(2):
            fh, fl = split(gathered[base + j])
            right = jnp.concatenate([fh, fl], axis=1)
            right = jnp.concatenate([right, right], axis=0)
            ah, al = split(tiles[base + j])
            left = jnp.concatenate([ah, al], axis=1)
            both = jnp.dot(left, right, preferred_element_type=F32)
            prods[j] = both[:, :128] + both[:, 128:]
        picks = []
        for j in range(2):
            live = live_s[0, base + j].astype(F32)
            target = row_s[0, base + j]
            picks.append([jnp.where(target == a, live, 0.0) for a in range(8)])
        for a in range(8):
            acc[a] = acc[a] + (prods[0] * picks[0][a] + prods[1] * picks[1][a])

    def duo(t, hh):
        for kk in range(2):
            take_all(block(slab(t), hh, kk))

        def side(i, carry):
            pair(slab(t * (2 * i - 1)), hh)
            return carry

        lax.fori_loop(0, 2, side, 0)

    other = 1 - k

    def ring(t):
        for c in range(CHUNKS):
            for kk, end in ((k, 8), (other, 7)):
                if t > end:
                    continue
                slot = block(slab(-t), h, kk)
                take(slot, c)
                if t % 2 == 0:
                    for hop in (2, 1):
                        if t + hop <= end:
                            send(slot, c, ahead[hop])
                send(slot, c, across)
                send(slot, c, partner)

    def crossed(t):
        for c in range(CHUNKS):
            for kk, end in ((k, 8), (other, 7)):
                if t > end or (t == 0 and kk is other):
                    continue
                slot = block(slab(-t), 1 - h, kk)
                take(slot, c)
                send(slot, c, partner)

    for c in range(CHUNKS):
        first(c, partner)
        for hop in (2, 1):
            first(c, ahead[hop])
        first(c, across)
    tell(0)
    acc[...] = jnp.zeros_like(acc)
    mine = block(z, h, other)
    for c in range(CHUNKS):
        take(mine, c)
        for hop in (2, 1):
            send(mine, c, ahead[hop])
    tile_copy.wait()
    row_copy.wait()
    live_copy.wait()
    ring(2)
    pl.semaphore_wait(ready.at[0], 2)
    tell(1)
    pair(z, h)
    ring(1)
    duo(2, h)
    for t in (4, 6):
        ring(t)
        duo(t - 3, h)
        ring(t - 1)
        duo(t, h)
    ring(8)
    ring(7)
    for t in (0, 2, 1, 4, 3):
        crossed(t)
    duo(5, h)
    take_all(block(z, 1 - h, other))
    pair(z, 1 - h)
    duo(2, 1 - h)
    duo(1, 1 - h)
    for t in (6, 5):
        crossed(t)
    duo(7, h)
    take_all(block(slab(8), h, other))
    pair(slab(8), h)
    for t in (4, 3, 6, 5):
        duo(t, 1 - h)
    crossed(8)
    crossed(7)
    duo(7, 1 - h)
    take_all(block(slab(8), 1 - h, other))
    pair(slab(8), 1 - h)

    pl.semaphore_wait(ready.at[1], 2)
    for dy, dx in ((2, 1), (1, 1), (3, 1), (0, 1), (2, 0), (1, 0), (3, 0)):
        to = ((y + dy) % ny) * 2 + (side_x + dx) % 2
        pltpu.make_async_remote_copy(
            src_ref=acc.at[to],
            dst_ref=incoming.at[dy * 2 + dx],
            send_sem=xs,
            recv_sem=xr,
            device_id=at_device(row, to),
            device_id_type=MESH,
        ).start()
    w_copy.wait()
    c_copy.wait()
    bias_copy.wait()
    node_copy.wait()
    wh, wl = split(wv[...])
    live = jnp.transpose(jnp.broadcast_to(node_v[...].astype(F32), (128, 128)))
    mask = jnp.concatenate([live, live], axis=1)
    arrived(incoming.at[pl.ds(1, nrep - 1)], xr)
    agg = acc[rep]
    for j in range(1, nrep):
        agg = agg + incoming[j]
    ah, al = split(agg)
    pre = jnp.dot(
        jnp.concatenate([ah, al], axis=1),
        jnp.concatenate([wh, wh], axis=0),
        preferred_element_type=F32,
    )
    pre = pre + jnp.dot(ah, wl, preferred_element_type=F32) + bias_v[...]
    sig = jax.nn.sigmoid(pre)
    av[...] = pre * sig * mask
    act_copy = pltpu.make_async_copy(av, act_out, osem.at[0])
    act_copy.start()
    grad = cv[...] * mask * sig * (1.0 + pre * (1.0 - sig))
    gh, gl = split(grad)
    along = (((0,), (0,)), ((), ()))
    wpart = lax.dot_general(
        jnp.concatenate([ah, al], axis=0),
        jnp.concatenate([gh, gh], axis=0),
        along,
        preferred_element_type=F32,
    ) + lax.dot_general(ah, gl, along, preferred_element_type=F32)
    part[pl.ds(0, 16)] = wpart[:, :128].reshape(16, 8, 128)
    part[pl.ds(16, 16)] = wpart[:, 128:].reshape(16, 8, 128)
    bias_sum = jnp.sum(grad, axis=0, keepdims=True)
    bpart[...] = jnp.zeros_like(bpart)
    bpart[0:1] = bias_sum[:, :128]
    bpart[1:2] = bias_sum[:, 128:]

    me = (row % 4) * nrep + rep

    x = h * 2 + side_x
    xs_at = [(x + dx) % 4 for dx in range(4)]
    row_at = [[z * 4 + xx // 2 * 2 + (k + dk) % 2 for dk in range(2)] for xx in xs_at]
    rep_at = [[(y + dy) % ny * 2 + xx % 2 for dy in range(4)] for xx in xs_at]

    def plane_peers():
        for j, (dx, dy, dk) in enumerate(PLANE):
            r, p = row_at[dx][dk], rep_at[dx][dy]
            yield j + 1, (r - z * 4) * nrep + p, at_device(r, p)

    z_far = sorted(range(1, nz), key=lambda j: -min(j, nz - j))

    def z_peers():
        for j in z_far:
            yield at_device((z + j) % nz * 4 + row % 4, rep)

    def copy_to(src, dst, at, dev):
        pltpu.make_async_remote_copy(
            src_ref=src,
            dst_ref=dst,
            send_sem=as_.at[at],
            recv_sem=ar.at[at],
            device_id=dev,
            device_id_type=MESH,
        ).start()

    def bcopy(src, dst, at, dev):
        return pltpu.make_async_remote_copy(
            src_ref=src,
            dst_ref=dst,
            send_sem=bs.at[at],
            recv_sem=br.at[at],
            device_id=dev,
            device_id_type=MESH,
        )

    for j, q, dev in plane_peers():
        copy_to(part.at[q], plane_in.at[j], 0, dev)

    @pl.when(me != 0)
    def _():
        bcopy(bpart, bplane.at[me], 0, at_device(z * 4, 0)).start()

    arrived(plane_in.at[pl.ds(1, nplane - 1)], ar.at[0])
    total = part[me]
    for j in range(1, nplane):
        total = total + plane_in[j]
    reduced[...] = total
    z_in[z] = total

    for dev in z_peers():
        copy_to(reduced, z_in.at[z], 1, dev)

    @pl.when(me == 0)
    def _():
        arrived(bplane.at[pl.ds(1, nplane - 1)], br.at[0])
        btotal = bpart[...]
        for j in range(1, nplane):
            btotal = btotal + bplane[j]
        breduced[...] = btotal
        bz[z] = btotal

        def balong(j, carry):
            zz = (z + j) % nz
            bcopy(breduced, bz.at[z], 1, at_device(zz * 4 + row % 4, rep)).start()
            return carry

        lax.fori_loop(1, nz, balong, 0)

    arrived(z_in.at[pl.ds(1, nz - 1)], ar.at[1])
    total = z_in[0]
    for j in range(1, nz):
        total = total + z_in[j]
    final[...] = total
    wsum[me] = total

    for j, q, dev in plane_peers():
        copy_to(final, wsum.at[me], 2, dev)

    @pl.when(me == 0)
    def _():
        arrived(bz.at[pl.ds(1, nz - 1)], br.at[1])
        btotal = bz[0]
        for j in range(1, nz):
            btotal = btotal + bz[j]
        bfinal[...] = btotal
        bsum[...] = btotal

        def bgather(j, carry):
            bcopy(bfinal, bsum, 2, at_device(z * 4 + j // nrep, j % nrep)).start()
            return carry

        lax.fori_loop(1, nplane, bgather, 0)

    arrived(wsum.at[pl.ds(1, nplane - 1)], ar.at[2])
    wg_out[:, :128] = wsum[pl.ds(0, 16)].reshape(128, 128)
    wg_out[:, 128:] = wsum[pl.ds(16, 16)].reshape(128, 128)

    @pl.when(me != 0)
    def _():
        arrived(bsum, br.at[2])
        arrived(bpart, bs.at[0])

    bg_out[:, :128] = bsum[0:1]
    bg_out[:, 128:] = bsum[1:2]

    @pl.when(me == 0)
    def _():
        arrived(bz.at[pl.ds(1, nz - 1)], bs.at[1])
        arrived(bplane.at[pl.ds(1, nplane - 1)], bs.at[2])

    sent = nz * 4 - 1
    arrived(gathered.at[pl.ds(0, sent)], ssem)
    arrived(incoming.at[pl.ds(1, nrep - 1)], xs)
    arrived(plane_in.at[pl.ds(1, nplane - 1)], as_.at[0])
    arrived(z_in.at[pl.ds(1, nz - 1)], as_.at[1])
    arrived(plane_in.at[pl.ds(1, nplane - 1)], as_.at[2])
    act_copy.wait()


def writer(act, wg, bg, act_out, wg_out, bg_out, sems):
    copies = [
        pltpu.make_async_copy(src, dst, sems.at[i])
        for i, (src, dst) in enumerate(((act, act_out), (wg, wg_out), (bg, bg_out)))
    ]
    for copy in copies:
        copy.start()
    for copy in copies:
        copy.wait()


def write_out(act, wg, bg):
    vmem = pl.BlockSpec(memory_space=pltpu.VMEM)
    hbm = pl.BlockSpec(memory_space=pltpu.HBM)
    act, wg, bg = pl.pallas_call(
        writer,
        out_shape=tuple(jax.ShapeDtypeStruct(x.shape, F32) for x in (act, wg, bg)),
        in_specs=[vmem] * 3,
        out_specs=(hbm,) * 3,
        scratch_shapes=[pltpu.SemaphoreType.DMA((3,))],
        compiler_params=pltpu.CompilerParams(vmem_limit_bytes=4 * 1024 * 1024),
    )(act, wg, bg)
    return act, wg, bg.reshape(256)


def local(features, weight, bias, adjacency, tile_row, tile_live, node_live, cotangent):
    count = adjacency.shape[2]
    nrep = lax.axis_size("rep")
    nplane = 4 * nrep
    nz = lax.axis_size("row") // 4
    hbm = pl.BlockSpec(memory_space=pltpu.HBM)
    vmem = pl.BlockSpec(memory_space=pltpu.VMEM)
    dma = pltpu.SemaphoreType.DMA
    act, wg, bg = pl.pallas_call(
        kernel,
        out_shape=(
            jax.ShapeDtypeStruct((128, 256), F32),
            jax.ShapeDtypeStruct((128, 256), F32),
            jax.ShapeDtypeStruct((1, 256), F32),
        ),
        in_specs=[hbm] * 8,
        out_specs=(hbm, vmem, vmem),
        scratch_shapes=[
            pltpu.VMEM((count, 128, 128), F32),
            pltpu.VMEM((count, 128, 128), F32),
            pltpu.VMEM((128, 256), F32),
            pltpu.VMEM((128, 256), F32),
            pltpu.VMEM((nrep, 128, 128), F32),
            pltpu.VMEM((2, 128, 128), F32),
            pltpu.VMEM((nrep, 128, 128), F32),
            pltpu.VMEM((128, 256), F32),
            pltpu.VMEM((nplane, 8, 128), F32),
            pltpu.VMEM((nplane, 8, 128), F32),
            pltpu.VMEM((8, 128), F32),
            pltpu.VMEM((nz, 8, 128), F32),
            pltpu.VMEM((8, 128), F32),
            pltpu.VMEM((nplane, 8, 128), F32),
            pltpu.VMEM((8, 128), F32),
            pltpu.VMEM((nplane, 8, 128), F32),
            pltpu.VMEM((8, 128), F32),
            pltpu.VMEM((nz, 8, 128), F32),
            pltpu.VMEM((8, 128), F32),
            pltpu.VMEM((8, 128), F32),
            pltpu.SMEM((1, count), jnp.int32),
            pltpu.SMEM((1, count), jnp.int32),
            pltpu.VMEM((1, 256), F32),
            pltpu.VMEM((1, 128), jnp.int32),
            pltpu.SemaphoreType.REGULAR((2,)),
            dma((7,)),
            dma,
            dma,
            dma((count, CHUNKS)),
            dma,
            dma,
            dma((3,)),
            dma((3,)),
            dma((3,)),
            dma((3,)),
            dma((1,)),
        ],
        compiler_params=pltpu.CompilerParams(
            collective_id=0, has_side_effects=True, vmem_limit_bytes=24 * 1024 * 1024
        ),
    )(
        *(
            pltpu.with_memory_space_constraint(x, pltpu.HBM)
            for x in (
                features,
                weight,
                bias.reshape(1, 256),
                adjacency.reshape(count, 128, 128),
                tile_row.reshape(1, count),
                tile_live.reshape(1, count),
                node_live.reshape(1, 128),
                cotangent,
            )
        )
    )
    return write_out(act, wg, bg)


def solution(mesh):
    placed = (
        P(("row", "rep"), None),
        P(),
        P(),
        P("row", "rep", None, None, None),
        P("row", "rep", None),
        P("row", "rep", None),
        P(("row", "rep")),
        P(("row", "rep"), None),
    )
    return jax.shard_map(
        local,
        mesh=mesh,
        in_specs=placed,
        out_specs=(P(("row", "rep"), None), P(), P()),
        check_vma=False,
    )
```

```python
import functools

import jax
import jax.numpy as jnp
from jax import lax
from jax.experimental import pallas as pl
from jax.experimental.pallas import tpu as pltpu
from jax.sharding import PartitionSpec as P

MESH = pl.DeviceIdType.MESH
F32 = jnp.float32
CHUNKS = 1
PLANE = sorted(
    ((dx, dy, dk) for dx in range(4) for dy in range(4) for dk in range(2)),
    key=lambda d: -(min(d[0], 4 - d[0]) + min(d[1], 4 - d[1])) * 2 - d[2],
)[:-1]
BF16 = jnp.bfloat16


def split(x):
    high = x.astype(BF16)
    return high, (x - high.astype(F32)).astype(BF16)


def arrived(ref, sem):
    pltpu.make_async_copy(ref, ref, sem).wait()


def kernel(
    feat,
    weight,
    bias,
    adj,
    trow,
    tlive,
    nlive,
    cot,
    act_out,
    wg_out,
    bg_out,
    gathered,
    tiles,
    wv,
    cv,
    acc,
    prods,
    incoming,
    av,
    part,
    plane_in,
    reduced,
    z_in,
    final,
    wsum,
    bpart,
    bplane,
    breduced,
    bz,
    bfinal,
    bsum,
    row_s,
    live_s,
    bias_v,
    node_v,
    ready,
    lsem,
    tsem,
    ssem,
    rsem,
    xs,
    xr,
    as_,
    ar,
    bs,
    br,
    osem,
):
    row = lax.axis_index("row")
    rep = lax.axis_index("rep")
    nz = lax.axis_size("row") // 4
    nrep = lax.axis_size("rep")
    nplane = 4 * nrep
    rows = 128 // CHUNKS
    z, h, k = row // 4, (row // 2) % 2, row % 2
    d = 1 - 2 * k

    def slab(t):
        return (z + t * d + nz) % nz

    def block(zz, hh, kk):
        return zz * 4 + hh * 2 + kk

    def at_device(r, p):
        return {"row": r, "rep": p}

    partner = at_device(block(z, h, 1 - k), rep)
    ahead = {t: at_device(block(slab(t), h, k), rep) for t in (1, 2)}
    across = at_device(block(z, 1 - h, k), rep)

    barrier = pltpu.get_barrier_semaphore()

    def greet(dev):
        pl.semaphore_signal(barrier, inc=1, device_id=dev, device_id_type=MESH)

    for t in (1, 2):
        greet(at_device(block(slab(-t), h, k), rep))
    greet(partner)
    greet(across)
    y, side_x = rep // 2, rep % 2
    ny = nrep // 2
    beside = [at_device(row, ((y + dy) % ny) * 2 + side_x) for dy in (1, 3)]
    for dev in beside:
        greet(dev)
    greet(at_device(row, y * 2 + 1 - side_x))

    own_copy = pltpu.make_async_copy(feat, gathered.at[row], lsem.at[0])
    own_copy.start()
    row_copy = pltpu.make_async_copy(trow, row_s, lsem.at[3])
    row_copy.start()
    live_copy = pltpu.make_async_copy(tlive, live_s, lsem.at[4])
    live_copy.start()
    tile_copy = pltpu.make_async_copy(adj, tiles, tsem)
    tile_copy.start()
    w_copy = pltpu.make_async_copy(weight, wv, lsem.at[1])
    w_copy.start()
    c_copy = pltpu.make_async_copy(cot, cv, lsem.at[2])
    c_copy.start()
    bias_copy = pltpu.make_async_copy(bias, bias_v, lsem.at[5])
    bias_copy.start()
    node_copy = pltpu.make_async_copy(nlive, node_v, lsem.at[6])
    node_copy.start()
    pl.semaphore_wait(barrier, 7)

    def tell(at):
        for dev in beside:
            pl.semaphore_signal(ready.at[at], inc=1, device_id=dev, device_id_type=MESH)

    own_copy.wait()

    def piece(slot, c):
        return gathered.at[slot, pl.ds(c * rows, rows)]

    def push(src, slot, c, dev):
        pltpu.make_async_remote_copy(
            src_ref=src,
            dst_ref=piece(slot, c),
            send_sem=ssem,
            recv_sem=rsem.at[slot, c],
            device_id=dev,
            device_id_type=MESH,
        ).start()

    def first(c, dev):
        push(piece(row, c), row, c, dev)

    def send(slot, c, dev):
        push(piece(slot, c), slot, c, dev)

    def take(slot, c):
        arrived(piece(slot, c), rsem.at[slot, c])

    def take_all(slot):
        for c in range(CHUNKS):
            take(slot, c)

    def multiply(zz, hh):
        base = zz * 4 + hh * 2
        for j in range(2):
            fh, fl = split(gathered[base + j])
            right = jnp.concatenate([fh, fl], axis=1)
            right = jnp.concatenate([right, right], axis=0)
            ah, al = split(tiles[base + j])
            left = jnp.concatenate([ah, al], axis=1)
            both = jnp.dot(left, right, preferred_element_type=F32)
            prods[j] = both[:, :128] + both[:, 128:]
        return [(row_s[0, base + j], live_s[0, base + j].astype(F32)) for j in range(2)]

    def add(rules, a):
        picks = [jnp.where(target == a, live, 0.0) for target, live in rules]
        acc[a] = acc[a] + (prods[0] * picks[0] + prods[1] * picks[1])

    def pair(zz, hh):
        rules = multiply(zz, hh)
        for a in range(8):
            add(rules, a)

    def duo(t, hh):
        for kk in range(2):
            take_all(block(slab(t), hh, kk))

        def side(i, carry):
            pair(slab(t * (2 * i - 1)), hh)
            return carry

        lax.fori_loop(0, 2, side, 0)

    other = 1 - k

    def ring(t):
        for c in range(CHUNKS):
            for kk, end in ((k, 8), (other, 7)):
                if t > end:
                    continue
                slot = block(slab(-t), h, kk)
                take(slot, c)
                send(slot, c, across)
                if t % 2 == 0:
                    for hop in (2, 1):
                        if t + hop <= end:
                            send(slot, c, ahead[hop])
                send(slot, c, partner)

    def crossed(t):
        for c in range(CHUNKS):
            for kk, end in ((k, 8), (other, 7)):
                if t > end or (t == 0 and kk is other):
                    continue
                slot = block(slab(-t), 1 - h, kk)
                take(slot, c)
                send(slot, c, partner)

    for c in range(CHUNKS):
        first(c, partner)
        for hop in (2, 1):
            first(c, ahead[hop])
        first(c, across)
    tell(0)
    acc[...] = jnp.zeros_like(acc)
    mine = block(z, h, other)
    for c in range(CHUNKS):
        take(mine, c)
        for hop in (2, 1):
            send(mine, c, ahead[hop])
    tile_copy.wait()
    row_copy.wait()
    live_copy.wait()
    ring(2)
    pl.semaphore_wait(ready.at[0], 2)
    tell(1)
    pair(z, h)
    ring(1)
    duo(2, h)
    for t in (4, 6):
        ring(t)
        duo(t - 3, h)
        ring(t - 1)
        duo(t, h)
    ring(8)
    ring(7)
    for t in (0, 2, 1, 4, 3):
        crossed(t)
    duo(5, h)
    take_all(block(z, 1 - h, other))
    pair(z, 1 - h)
    duo(2, 1 - h)
    duo(1, 1 - h)
    for t in (6, 5):
        crossed(t)
    duo(7, h)
    take_all(block(slab(8), h, other))
    pair(slab(8), h)
    for t in (4, 3, 6, 5):
        duo(t, 1 - h)
    crossed(8)
    crossed(7)
    pair(slab(-7), 1 - h)
    for kk in range(2):
        take_all(block(slab(7), 1 - h, kk))
    pair(slab(7), 1 - h)
    take_all(block(slab(8), 1 - h, other))

    pl.semaphore_wait(ready.at[1], 2)
    last = multiply(slab(8), 1 - h)
    for dy, dx in ((2, 1), (1, 1), (3, 1), (0, 1), (2, 0), (1, 0), (3, 0)):
        to = ((y + dy) % ny) * 2 + (side_x + dx) % 2
        add(last, to)
        pltpu.make_async_remote_copy(
            src_ref=acc.at[to],
            dst_ref=incoming.at[dy * 2 + dx],
            send_sem=xs,
            recv_sem=xr.at[dy * 2 + dx],
            device_id=at_device(row, to),
            device_id_type=MESH,
        ).start()
    add(last, rep)
    w_copy.wait()
    c_copy.wait()
    bias_copy.wait()
    node_copy.wait()
    wh, wl = split(wv[...])
    live = jnp.transpose(jnp.broadcast_to(node_v[...].astype(F32), (128, 128)))
    mask = jnp.concatenate([live, live], axis=1)
    agg = acc[rep]
    for j in (4, 2, 6, 1, 3, 7, 5):
        arrived(incoming.at[j], xr.at[j])
        agg = agg + incoming[j]
    ah, al = split(agg)
    pre = jnp.dot(
        jnp.concatenate([ah, al], axis=1),
        jnp.concatenate([wh, wh], axis=0),
        preferred_element_type=F32,
    )
    pre = pre + jnp.dot(ah, wl, preferred_element_type=F32) + bias_v[...]
    sig = jax.nn.sigmoid(pre)
    av[...] = pre * sig * mask
    act_copy = pltpu.make_async_copy(av, act_out, osem.at[0])
    act_copy.start()
    grad = cv[...] * mask * sig * (1.0 + pre * (1.0 - sig))
    gh, gl = split(grad)
    along = (((0,), (0,)), ((), ()))
    wpart = lax.dot_general(
        jnp.concatenate([ah, al], axis=0),
        jnp.concatenate([gh, gh], axis=0),
        along,
        preferred_element_type=F32,
    ) + lax.dot_general(ah, gl, along, preferred_element_type=F32)
    part[pl.ds(0, 16)] = wpart[:, :128].reshape(16, 8, 128)
    part[pl.ds(16, 16)] = wpart[:, 128:].reshape(16, 8, 128)
    bias_sum = jnp.sum(grad, axis=0, keepdims=True)
    bpart[...] = jnp.zeros_like(bpart)
    bpart[0:1] = bias_sum[:, :128]
    bpart[1:2] = bias_sum[:, 128:]

    me = (row % 4) * nrep + rep

    x = h * 2 + side_x
    xs_at = [(x + dx) % 4 for dx in range(4)]
    row_at = [[z * 4 + xx // 2 * 2 + (k + dk) % 2 for dk in range(2)] for xx in xs_at]
    rep_at = [[(y + dy) % ny * 2 + xx % 2 for dy in range(4)] for xx in xs_at]

    def plane_peers():
        for j, (dx, dy, dk) in enumerate(PLANE):
            r, p = row_at[dx][dk], rep_at[dx][dy]
            yield j + 1, (r - z * 4) * nrep + p, at_device(r, p)

    z_far = sorted(range(1, nz), key=lambda j: -min(j, nz - j))

    def z_peers():
        for j in z_far:
            yield at_device((z + j) % nz * 4 + row % 4, rep)

    def copy_to(src, dst, at, dev):
        pltpu.make_async_remote_copy(
            src_ref=src,
            dst_ref=dst,
            send_sem=as_.at[at],
            recv_sem=ar.at[at],
            device_id=dev,
            device_id_type=MESH,
        ).start()

    def bcopy(src, dst, at, dev):
        return pltpu.make_async_remote_copy(
            src_ref=src,
            dst_ref=dst,
            send_sem=bs.at[at],
            recv_sem=br.at[at],
            device_id=dev,
            device_id_type=MESH,
        )

    for j, q, dev in plane_peers():
        copy_to(part.at[q], plane_in.at[j], 0, dev)

    @pl.when(me != 0)
    def _():
        bcopy(bpart, bplane.at[me], 0, at_device(z * 4, 0)).start()

    arrived(plane_in.at[pl.ds(1, nplane - 1)], ar.at[0])
    total = part[me]
    for j in range(1, nplane):
        total = total + plane_in[j]
    reduced[...] = total
    z_in[z] = total

    for dev in z_peers():
        copy_to(reduced, z_in.at[z], 1, dev)

    @pl.when(me == 0)
    def _():
        arrived(bplane.at[pl.ds(1, nplane - 1)], br.at[0])
        btotal = bpart[...]
        for j in range(1, nplane):
            btotal = btotal + bplane[j]
        breduced[...] = btotal
        bz[z] = btotal

        def balong(j, carry):
            zz = (z + j) % nz
            bcopy(breduced, bz.at[z], 1, at_device(zz * 4 + row % 4, rep)).start()
            return carry

        lax.fori_loop(1, nz, balong, 0)

    arrived(z_in.at[pl.ds(1, nz - 1)], ar.at[1])
    total = z_in[0]
    for j in range(1, nz):
        total = total + z_in[j]
    final[...] = total
    wsum[me] = total

    for j, q, dev in plane_peers():
        copy_to(final, wsum.at[me], 2, dev)

    @pl.when(me == 0)
    def _():
        arrived(bz.at[pl.ds(1, nz - 1)], br.at[1])
        btotal = bz[0]
        for j in range(1, nz):
            btotal = btotal + bz[j]
        bfinal[...] = btotal
        bsum[...] = btotal

        def bgather(j, carry):
            bcopy(bfinal, bsum, 2, at_device(z * 4 + j // nrep, j % nrep)).start()
            return carry

        lax.fori_loop(1, nplane, bgather, 0)

    arrived(wsum.at[pl.ds(1, nplane - 1)], ar.at[2])
    wg_out[:, :128] = wsum[pl.ds(0, 16)].reshape(128, 128)
    wg_out[:, 128:] = wsum[pl.ds(16, 16)].reshape(128, 128)

    @pl.when(me != 0)
    def _():
        arrived(bsum, br.at[2])
        arrived(bpart, bs.at[0])

    bg_out[:, :128] = bsum[0:1]
    bg_out[:, 128:] = bsum[1:2]

    @pl.when(me == 0)
    def _():
        arrived(bz.at[pl.ds(1, nz - 1)], bs.at[1])
        arrived(bplane.at[pl.ds(1, nplane - 1)], bs.at[2])

    sent = nz * 4 - 1
    arrived(gathered.at[pl.ds(0, sent)], ssem)
    arrived(incoming.at[pl.ds(1, nrep - 1)], xs)
    arrived(plane_in.at[pl.ds(1, nplane - 1)], as_.at[0])
    arrived(z_in.at[pl.ds(1, nz - 1)], as_.at[1])
    arrived(plane_in.at[pl.ds(1, nplane - 1)], as_.at[2])
    act_copy.wait()


def writer(act, wg, bg, act_out, wg_out, bg_out, sems):
    copies = [
        pltpu.make_async_copy(src, dst, sems.at[i])
        for i, (src, dst) in enumerate(((act, act_out), (wg, wg_out), (bg, bg_out)))
    ]
    for copy in copies:
        copy.start()
    for copy in copies:
        copy.wait()


def write_out(act, wg, bg):
    vmem = pl.BlockSpec(memory_space=pltpu.VMEM)
    hbm = pl.BlockSpec(memory_space=pltpu.HBM)
    act, wg, bg = pl.pallas_call(
        writer,
        out_shape=tuple(jax.ShapeDtypeStruct(x.shape, F32) for x in (act, wg, bg)),
        in_specs=[vmem] * 3,
        out_specs=(hbm,) * 3,
        scratch_shapes=[pltpu.SemaphoreType.DMA((3,))],
        compiler_params=pltpu.CompilerParams(vmem_limit_bytes=4 * 1024 * 1024),
    )(act, wg, bg)
    return act, wg, bg.reshape(256)


def local(features, weight, bias, adjacency, tile_row, tile_live, node_live, cotangent):
    count = adjacency.shape[2]
    nrep = lax.axis_size("rep")
    nplane = 4 * nrep
    nz = lax.axis_size("row") // 4
    hbm = pl.BlockSpec(memory_space=pltpu.HBM)
    vmem = pl.BlockSpec(memory_space=pltpu.VMEM)
    dma = pltpu.SemaphoreType.DMA
    act, wg, bg = pl.pallas_call(
        kernel,
        out_shape=(
            jax.ShapeDtypeStruct((128, 256), F32),
            jax.ShapeDtypeStruct((128, 256), F32),
            jax.ShapeDtypeStruct((1, 256), F32),
        ),
        in_specs=[hbm] * 8,
        out_specs=(hbm, vmem, vmem),
        scratch_shapes=[
            pltpu.VMEM((count, 128, 128), F32),
            pltpu.VMEM((count, 128, 128), F32),
            pltpu.VMEM((128, 256), F32),
            pltpu.VMEM((128, 256), F32),
            pltpu.VMEM((nrep, 128, 128), F32),
            pltpu.VMEM((2, 128, 128), F32),
            pltpu.VMEM((nrep, 128, 128), F32),
            pltpu.VMEM((128, 256), F32),
            pltpu.VMEM((nplane, 8, 128), F32),
            pltpu.VMEM((nplane, 8, 128), F32),
            pltpu.VMEM((8, 128), F32),
            pltpu.VMEM((nz, 8, 128), F32),
            pltpu.VMEM((8, 128), F32),
            pltpu.VMEM((nplane, 8, 128), F32),
            pltpu.VMEM((8, 128), F32),
            pltpu.VMEM((nplane, 8, 128), F32),
            pltpu.VMEM((8, 128), F32),
            pltpu.VMEM((nz, 8, 128), F32),
            pltpu.VMEM((8, 128), F32),
            pltpu.VMEM((8, 128), F32),
            pltpu.SMEM((1, count), jnp.int32),
            pltpu.SMEM((1, count), jnp.int32),
            pltpu.VMEM((1, 256), F32),
            pltpu.VMEM((1, 128), jnp.int32),
            pltpu.SemaphoreType.REGULAR((2,)),
            dma((7,)),
            dma,
            dma,
            dma((count, CHUNKS)),
            dma,
            dma((nrep,)),
            dma((3,)),
            dma((3,)),
            dma((3,)),
            dma((3,)),
            dma((1,)),
        ],
        compiler_params=pltpu.CompilerParams(
            collective_id=0, has_side_effects=True, vmem_limit_bytes=24 * 1024 * 1024
        ),
    )(
        *(
            pltpu.with_memory_space_constraint(x, pltpu.HBM)
            for x in (
                features,
                weight,
                bias.reshape(1, 256),
                adjacency.reshape(count, 128, 128),
                tile_row.reshape(1, count),
                tile_live.reshape(1, count),
                node_live.reshape(1, 128),
                cotangent,
            )
        )
    )
    return write_out(act, wg, bg)


def solution(mesh):
    placed = (
        P(("row", "rep"), None),
        P(),
        P(),
        P("row", "rep", None, None, None),
        P("row", "rep", None),
        P("row", "rep", None),
        P(("row", "rep")),
        P(("row", "rep"), None),
    )
    return jax.shard_map(
        local,
        mesh=mesh,
        in_specs=placed,
        out_specs=(P(("row", "rep"), None), P(), P()),
        check_vma=False,
    )
```

```python
import functools

import jax
import jax.numpy as jnp
from jax import lax
from jax.experimental import pallas as pl
from jax.experimental.pallas import tpu as pltpu
from jax.sharding import PartitionSpec as P

MESH = pl.DeviceIdType.MESH
F32 = jnp.float32
CHUNKS = 1
PLANE = sorted(
    ((dx, dy, dk) for dx in range(4) for dy in range(4) for dk in range(2)),
    key=lambda d: -(min(d[0], 4 - d[0]) + min(d[1], 4 - d[1])) * 2 - d[2],
)[:-1]
BF16 = jnp.bfloat16


def split(x):
    high = x.astype(BF16)
    return high, (x - high.astype(F32)).astype(BF16)


def arrived(ref, sem):
    pltpu.make_async_copy(ref, ref, sem).wait()


def kernel(
    feat,
    weight,
    bias,
    adj,
    trow,
    tlive,
    nlive,
    cot,
    act_out,
    wg_out,
    bg_out,
    gathered,
    tiles,
    wv,
    cv,
    acc,
    prods,
    incoming,
    av,
    part,
    plane_in,
    reduced,
    z_in,
    final,
    wsum,
    bpart,
    bplane,
    row_s,
    live_s,
    bias_v,
    node_v,
    ready,
    lsem,
    tsem,
    ssem,
    rsem,
    xs,
    xr,
    as_,
    ar,
    bs,
    br,
    osem,
):
    row = lax.axis_index("row")
    rep = lax.axis_index("rep")
    nz = lax.axis_size("row") // 4
    nrep = lax.axis_size("rep")
    nplane = 4 * nrep
    rows = 128 // CHUNKS
    z, h, k = row // 4, (row // 2) % 2, row % 2
    d = 1 - 2 * k

    def slab(t):
        return (z + t * d + nz) % nz

    def block(zz, hh, kk):
        return zz * 4 + hh * 2 + kk

    def at_device(r, p):
        return {"row": r, "rep": p}

    partner = at_device(block(z, h, 1 - k), rep)
    ahead = {t: at_device(block(slab(t), h, k), rep) for t in (1, 2)}
    across = at_device(block(z, 1 - h, k), rep)

    barrier = pltpu.get_barrier_semaphore()

    def greet(dev):
        pl.semaphore_signal(barrier, inc=1, device_id=dev, device_id_type=MESH)

    for t in (1, 2):
        greet(at_device(block(slab(-t), h, k), rep))
    greet(partner)
    greet(across)
    y, side_x = rep // 2, rep % 2
    ny = nrep // 2
    beside = [at_device(row, ((y + dy) % ny) * 2 + side_x) for dy in (1, 3)]
    for dev in beside:
        greet(dev)
    greet(at_device(row, y * 2 + 1 - side_x))

    own_copy = pltpu.make_async_copy(feat, gathered.at[row], lsem.at[0])
    own_copy.start()
    row_copy = pltpu.make_async_copy(trow, row_s, lsem.at[3])
    row_copy.start()
    live_copy = pltpu.make_async_copy(tlive, live_s, lsem.at[4])
    live_copy.start()
    tile_copy = pltpu.make_async_copy(adj, tiles, tsem)
    tile_copy.start()
    w_copy = pltpu.make_async_copy(weight, wv, lsem.at[1])
    w_copy.start()
    c_copy = pltpu.make_async_copy(cot, cv, lsem.at[2])
    c_copy.start()
    bias_copy = pltpu.make_async_copy(bias, bias_v, lsem.at[5])
    bias_copy.start()
    node_copy = pltpu.make_async_copy(nlive, node_v, lsem.at[6])
    node_copy.start()
    pl.semaphore_wait(barrier, 7)

    def tell(at):
        for dev in beside:
            pl.semaphore_signal(ready.at[at], inc=1, device_id=dev, device_id_type=MESH)

    own_copy.wait()

    def piece(slot, c):
        return gathered.at[slot, pl.ds(c * rows, rows)]

    def push(src, slot, c, dev):
        pltpu.make_async_remote_copy(
            src_ref=src,
            dst_ref=piece(slot, c),
            send_sem=ssem,
            recv_sem=rsem.at[slot, c],
            device_id=dev,
            device_id_type=MESH,
        ).start()

    def first(c, dev):
        push(piece(row, c), row, c, dev)

    def send(slot, c, dev):
        push(piece(slot, c), slot, c, dev)

    def take(slot, c):
        arrived(piece(slot, c), rsem.at[slot, c])

    def take_all(slot):
        for c in range(CHUNKS):
            take(slot, c)

    def pair(zz, hh):
        base = zz * 4 + hh * 2
        for j in range(2):
            fh, fl = split(gathered[base + j])
            right = jnp.concatenate([fh, fl], axis=1)
            right = jnp.concatenate([right, right], axis=0)
            ah, al = split(tiles[base + j])
            left = jnp.concatenate([ah, al], axis=1)
            both = jnp.dot(left, right, preferred_element_type=F32)
            prods[j] = both[:, :128] + both[:, 128:]
        picks = []
        for j in range(2):
            live = live_s[0, base + j].astype(F32)
            target = row_s[0, base + j]
            picks.append([jnp.where(target == a, live, 0.0) for a in range(8)])
        for a in range(8):
            acc[a] = acc[a] + (prods[0] * picks[0][a] + prods[1] * picks[1][a])

    def duo(t, hh):
        for kk in range(2):
            take_all(block(slab(t), hh, kk))

        def side(i, carry):
            pair(slab(t * (2 * i - 1)), hh)
            return carry

        lax.fori_loop(0, 2, side, 0)

    other = 1 - k

    def ring(t):
        for c in range(CHUNKS):
            for kk, end in ((k, 8), (other, 7)):
                if t > end:
                    continue
                slot = block(slab(-t), h, kk)
                take(slot, c)
                if t % 2 == 0:
                    for hop in (2, 1):
                        if t + hop <= end:
                            send(slot, c, ahead[hop])
                send(slot, c, across)
                send(slot, c, partner)

    def crossed(t):
        for c in range(CHUNKS):
            for kk, end in ((k, 8), (other, 7)):
                if t > end or (t == 0 and kk is other):
                    continue
                slot = block(slab(-t), 1 - h, kk)
                take(slot, c)
                send(slot, c, partner)

    for c in range(CHUNKS):
        first(c, partner)
        for hop in (2, 1):
            first(c, ahead[hop])
        first(c, across)
    tell(0)
    acc[...] = jnp.zeros_like(acc)
    mine = block(z, h, other)
    for c in range(CHUNKS):
        take(mine, c)
        for hop in (2, 1):
            send(mine, c, ahead[hop])
    tile_copy.wait()
    row_copy.wait()
    live_copy.wait()
    ring(2)
    pl.semaphore_wait(ready.at[0], 2)
    tell(1)
    pair(z, h)
    ring(1)
    duo(2, h)
    for t in (4, 6):
        ring(t)
        duo(t - 3, h)
        ring(t - 1)
        duo(t, h)
    ring(8)
    ring(7)
    for t in (0, 2, 1, 4, 3):
        crossed(t)
    duo(5, h)
    take_all(block(z, 1 - h, other))
    pair(z, 1 - h)
    duo(2, 1 - h)
    duo(1, 1 - h)
    for t in (6, 5):
        crossed(t)
    duo(7, h)
    take_all(block(slab(8), h, other))
    pair(slab(8), h)
    for t in (4, 3, 6, 5):
        duo(t, 1 - h)
    crossed(8)
    crossed(7)
    duo(7, 1 - h)
    take_all(block(slab(8), 1 - h, other))
    pair(slab(8), 1 - h)

    pl.semaphore_wait(ready.at[1], 2)
    for dy, dx in ((2, 1), (1, 1), (3, 1), (0, 1), (2, 0), (1, 0), (3, 0)):
        to = ((y + dy) % ny) * 2 + (side_x + dx) % 2
        pltpu.make_async_remote_copy(
            src_ref=acc.at[to],
            dst_ref=incoming.at[dy * 2 + dx],
            send_sem=xs,
            recv_sem=xr,
            device_id=at_device(row, to),
            device_id_type=MESH,
        ).start()
    w_copy.wait()
    c_copy.wait()
    bias_copy.wait()
    node_copy.wait()
    wh, wl = split(wv[...])
    live = jnp.transpose(jnp.broadcast_to(node_v[...].astype(F32), (128, 128)))
    mask = jnp.concatenate([live, live], axis=1)
    arrived(incoming.at[pl.ds(1, nrep - 1)], xr)
    agg = acc[rep]
    for j in range(1, nrep):
        agg = agg + incoming[j]
    ah, al = split(agg)
    pre = jnp.dot(
        jnp.concatenate([ah, al], axis=1),
        jnp.concatenate([wh, wh], axis=0),
        preferred_element_type=F32,
    )
    pre = pre + jnp.dot(ah, wl, preferred_element_type=F32) + bias_v[...]
    sig = jax.nn.sigmoid(pre)
    av[...] = pre * sig * mask
    act_copy = pltpu.make_async_copy(av, act_out, osem.at[0])
    act_copy.start()
    grad = cv[...] * mask * sig * (1.0 + pre * (1.0 - sig))
    gh, gl = split(grad)
    along = (((0,), (0,)), ((), ()))
    wpart = lax.dot_general(
        jnp.concatenate([ah, al], axis=0),
        jnp.concatenate([gh, gh], axis=0),
        along,
        preferred_element_type=F32,
    ) + lax.dot_general(ah, gl, along, preferred_element_type=F32)
    part[pl.ds(0, 16)] = wpart[:, :128].reshape(16, 8, 128)
    part[pl.ds(16, 16)] = wpart[:, 128:].reshape(16, 8, 128)
    bias_sum = jnp.sum(grad, axis=0, keepdims=True)
    bpart[...] = jnp.zeros_like(bpart)
    bpart[0:1] = bias_sum[:, :128]
    bpart[1:2] = bias_sum[:, 128:]

    me = (row % 4) * nrep + rep

    x = h * 2 + side_x
    xs_at = [(x + dx) % 4 for dx in range(4)]
    row_at = [[z * 4 + xx // 2 * 2 + (k + dk) % 2 for dk in range(2)] for xx in xs_at]
    rep_at = [[(y + dy) % ny * 2 + xx % 2 for dy in range(4)] for xx in xs_at]

    def plane_peers():
        for j, (dx, dy, dk) in enumerate(PLANE):
            r, p = row_at[dx][dk], rep_at[dx][dy]
            yield j + 1, (r - z * 4) * nrep + p, at_device(r, p)

    z_far = sorted(range(1, nz), key=lambda j: -min(j, nz - j))

    def z_peers():
        for j in z_far:
            yield at_device((z + j) % nz * 4 + row % 4, rep)

    def copy_to(src, dst, at, dev):
        pltpu.make_async_remote_copy(
            src_ref=src,
            dst_ref=dst,
            send_sem=as_.at[at],
            recv_sem=ar.at[at],
            device_id=dev,
            device_id_type=MESH,
        ).start()

    def bcopy(src, dst, at, dev):
        return pltpu.make_async_remote_copy(
            src_ref=src,
            dst_ref=dst,
            send_sem=bs.at[at],
            recv_sem=br.at[at],
            device_id=dev,
            device_id_type=MESH,
        )

    for j, q, dev in plane_peers():
        copy_to(part.at[q], plane_in.at[j], 0, dev)

    @pl.when(me != 0)
    def _():
        bcopy(bpart, bplane.at[me], 0, at_device(z * 4, 0)).start()

    arrived(plane_in.at[pl.ds(1, nplane - 1)], ar.at[0])
    total = part[me]
    for j in range(1, nplane):
        total = total + plane_in[j]
    reduced[1] = total
    z_in[z, 1] = total

    @pl.when(me != 0)
    def _():
        for dev in z_peers():
            copy_to(reduced.at[1], z_in.at[z, 1], 1, dev)

    @pl.when(me == 0)
    def _():
        arrived(bplane.at[pl.ds(1, nplane - 1)], br.at[0])
        extra = bpart[...]
        for j in range(1, nplane):
            extra = extra + bplane[j]
        reduced[0] = extra
        z_in[z, 0] = extra
        for dev in z_peers():
            copy_to(reduced, z_in.at[z], 1, dev)

    def z_done(sem):
        @pl.when(me != 0)
        def _():
            arrived(plane_in.at[pl.ds(1, nz - 1)], sem)

        @pl.when(me == 0)
        def _():
            arrived(z_in.at[pl.ds(1, nz - 1)], sem)

    z_done(ar.at[1])
    total = z_in[0, 1]
    for j in range(1, nz):
        total = total + z_in[j, 1]
    final[1] = total
    wsum[me + 1] = total

    @pl.when(me != 0)
    def _():
        for _, _, dev in plane_peers():
            copy_to(final.at[1], wsum.at[me + 1], 2, dev)
        arrived(wsum.at[pl.ds(0, nplane)], ar.at[2])
        arrived(plane_in.at[pl.ds(1, nplane - 1)], as_.at[2])
        arrived(bpart, bs.at[0])

    @pl.when(me == 0)
    def _():
        extra = z_in[0, 0]
        for j in range(1, nz):
            extra = extra + z_in[j, 0]
        final[0] = extra
        wsum[0] = extra
        for _, _, dev in plane_peers():
            copy_to(final, wsum.at[pl.ds(0, 2)], 2, dev)
        arrived(plane_in.at[pl.ds(1, nplane - 1)], ar.at[2])
        arrived(wsum.at[pl.ds(0, nplane - 1)], as_.at[2])
        arrived(wsum.at[pl.ds(0, nplane - 1)], as_.at[2])

    wg_out[:, :128] = wsum[pl.ds(1, 16)].reshape(128, 128)
    wg_out[:, 128:] = wsum[pl.ds(17, 16)].reshape(128, 128)
    bg_out[:, :128] = wsum[0, 0:1]
    bg_out[:, 128:] = wsum[0, 1:2]

    z_done(as_.at[1])
    sent = nz * 4 - 1
    arrived(gathered.at[pl.ds(0, sent)], ssem)
    arrived(incoming.at[pl.ds(1, nrep - 1)], xs)
    arrived(plane_in.at[pl.ds(1, nplane - 1)], as_.at[0])
    act_copy.wait()


def writer(act, wg, bg, act_out, wg_out, bg_out, sems):
    copies = [
        pltpu.make_async_copy(src, dst, sems.at[i])
        for i, (src, dst) in enumerate(((act, act_out), (wg, wg_out), (bg, bg_out)))
    ]
    for copy in copies:
        copy.start()
    for copy in copies:
        copy.wait()


def write_out(act, wg, bg):
    vmem = pl.BlockSpec(memory_space=pltpu.VMEM)
    hbm = pl.BlockSpec(memory_space=pltpu.HBM)
    act, wg, bg = pl.pallas_call(
        writer,
        out_shape=tuple(jax.ShapeDtypeStruct(x.shape, F32) for x in (act, wg, bg)),
        in_specs=[vmem] * 3,
        out_specs=(hbm,) * 3,
        scratch_shapes=[pltpu.SemaphoreType.DMA((3,))],
        compiler_params=pltpu.CompilerParams(vmem_limit_bytes=4 * 1024 * 1024),
    )(act, wg, bg)
    return act, wg, bg.reshape(256)


def local(features, weight, bias, adjacency, tile_row, tile_live, node_live, cotangent):
    count = adjacency.shape[2]
    nrep = lax.axis_size("rep")
    nplane = 4 * nrep
    nz = lax.axis_size("row") // 4
    hbm = pl.BlockSpec(memory_space=pltpu.HBM)
    vmem = pl.BlockSpec(memory_space=pltpu.VMEM)
    dma = pltpu.SemaphoreType.DMA
    act, wg, bg = pl.pallas_call(
        kernel,
        out_shape=(
            jax.ShapeDtypeStruct((128, 256), F32),
            jax.ShapeDtypeStruct((128, 256), F32),
            jax.ShapeDtypeStruct((1, 256), F32),
        ),
        in_specs=[hbm] * 8,
        out_specs=(hbm, vmem, vmem),
        scratch_shapes=[
            pltpu.VMEM((count, 128, 128), F32),
            pltpu.VMEM((count, 128, 128), F32),
            pltpu.VMEM((128, 256), F32),
            pltpu.VMEM((128, 256), F32),
            pltpu.VMEM((nrep, 128, 128), F32),
            pltpu.VMEM((2, 128, 128), F32),
            pltpu.VMEM((nrep, 128, 128), F32),
            pltpu.VMEM((128, 256), F32),
            pltpu.VMEM((nplane, 8, 128), F32),
            pltpu.VMEM((nplane, 8, 128), F32),
            pltpu.VMEM((2, 8, 128), F32),
            pltpu.VMEM((nz, 2, 8, 128), F32),
            pltpu.VMEM((2, 8, 128), F32),
            pltpu.VMEM((nplane + 1, 8, 128), F32),
            pltpu.VMEM((8, 128), F32),
            pltpu.VMEM((nplane, 8, 128), F32),
            pltpu.SMEM((1, count), jnp.int32),
            pltpu.SMEM((1, count), jnp.int32),
            pltpu.VMEM((1, 256), F32),
            pltpu.VMEM((1, 128), jnp.int32),
            pltpu.SemaphoreType.REGULAR((2,)),
            dma((7,)),
            dma,
            dma,
            dma((count, CHUNKS)),
            dma,
            dma,
            dma((3,)),
            dma((3,)),
            dma((1,)),
            dma((1,)),
            dma((1,)),
        ],
        compiler_params=pltpu.CompilerParams(
            collective_id=0, has_side_effects=True, vmem_limit_bytes=24 * 1024 * 1024
        ),
    )(
        *(
            pltpu.with_memory_space_constraint(x, pltpu.HBM)
            for x in (
                features,
                weight,
                bias.reshape(1, 256),
                adjacency.reshape(count, 128, 128),
                tile_row.reshape(1, count),
                tile_live.reshape(1, count),
                node_live.reshape(1, 128),
                cotangent,
            )
        )
    )
    return write_out(act, wg, bg)


def solution(mesh):
    placed = (
        P(("row", "rep"), None),
        P(),
        P(),
        P("row", "rep", None, None, None),
        P("row", "rep", None),
        P("row", "rep", None),
        P(("row", "rep")),
        P(("row", "rep"), None),
    )
    return jax.shard_map(
        local,
        mesh=mesh,
        in_specs=placed,
        out_specs=(P(("row", "rep"), None), P(), P()),
        check_vma=False,
    )
```
